32 devices in a mesh: groups: 2 (over y), row: 16 (over z, x, core).
Axes of the slice: x: 2, y: 2, z: 4, core: 2. Of those that a mesh axis runs over, the one named last changes fastest.
Arguments:
- layer_input: bfloat16 [8192, 512], P('row', 'groups'), parts along dimension 1, may hold values from -6 to 6
- output_grad: bfloat16 [8192, 512], P('row', 'groups'), parts along dimension 1, may hold values from -1.5 to 1.5
- gate_weight: bfloat16 [28672, 8192], P(('groups', 'row')), parts along dimension 0, may hold values from -0.09375 to 0.09375
- up_weight: bfloat16 [28672, 8192], P(('groups', 'row')), parts along dimension 0, may hold values from -0.09375 to 0.09375
- down_weight: bfloat16 [28672, 8192], P(('groups', 'row')), parts along dimension 0, may hold values from -0.046875 to 0.046875
Outputs:
- input_grad: bfloat16 [8192, 512], P('row', 'groups'), parts along dimension 1
- gate_grad: bfloat16 [28672, 8192], P(('groups', 'row')), parts along dimension 0
- up_grad: bfloat16 [28672, 8192], P(('groups', 'row')), parts along dimension 0
- down_grad: bfloat16 [28672, 8192], P(('groups', 'row')), parts along dimension 0
The draws below stay inside these ranges and needn't reach their ends.
There are 2 independent parts, one for each index of `groups`. The reference program is written for one: setup_inputs(seed, part) draws one part's arguments, and reference() takes and returns one part's arrays. A program takes and returns all parts, laid end to end along the dimension named above; each array names one. Nothing has to cross between parts.
All inputs are finite; a program needn't handle non-finite values.
Results may differ from the reference program's by a relative error of at most 0.0049.
Values may be sent and summed in bfloat16 or wider, within the bound.
A program may use at most 192 MiB of HBM per device.

```python
import jax
import jax.numpy as jnp

D = 8192
FF = 14336
TOKENS = 256


def raised(drawn, own_key, source, target, blocks, factor):
    def block_of(position):
        return (jnp.arange(drawn.shape[position]) // (drawn.shape[position] // blocks)).reshape((-1,) + (1,) * (drawn.ndim - 1 - position))

    one_side = jax.random.permutation(own_key, blocks)[block_of(target)]
    far = (block_of(target) + blocks // 2) % blocks
    return jnp.where((block_of(source) == one_side) | (block_of(source) == far), factor * drawn, drawn)


def block_scale(stream_key, shape, cuts, least, top_value):
    def one(dim, shards_of):
        steps = jax.random.uniform(jax.random.fold_in(jax.random.fold_in(stream_key, 6), dim), (shards_of,), jnp.float32, least / len(cuts), top_value / len(cuts))
        return jnp.repeat(jnp.exp(steps), shape[dim] // shards_of).reshape((-1,) + (1,) * (len(shape) - dim - 1))

    factor_of = one(*cuts[0])
    for cut in cuts[1:]:
        factor_of = factor_of * one(*cut)
    return factor_of


def noise(stream_key, extent, width, limit, split=(), kind=jnp.bfloat16):
    loudness = block_scale(stream_key, extent, split, -0.22, 0.18) if split else 1.0
    entries = jax.random.normal(stream_key, extent, jnp.float32) * width * loudness
    return jnp.minimum(jnp.maximum(entries, -limit), limit).astype(kind)


def heavy_noise(key, extent, scale, reach, shards, heavy, dtype=jnp.bfloat16):
    result = scale * jax.random.normal(key, extent, jnp.float32)
    if shards:
        result = result * block_scale(key, extent, shards, -0.22, 0.18)
    return jnp.clip(raised(result, jax.random.fold_in(key, 3), *heavy), -reach, reach).astype(dtype)


def setup_inputs(seed: int = 0, part: int = 0) -> dict:
    keys = jax.random.split(jax.random.key(seed), 6)
    own_keys = jax.random.split(jax.random.fold_in(keys[5], part), 6)
    layer_input = noise(own_keys[0], (D, TOKENS), 1.0, 6.0, ((0, 16),))
    output_grad = noise(own_keys[1], (D, TOKENS), 0.25, 1.5, ((0, 16),))
    gate_weight = heavy_noise(own_keys[2], (FF, D), D ** -0.5, 0.09375, ((0, 16),), (0, 1, 16, 2.0))
    up_weight = heavy_noise(own_keys[3], (FF, D), D ** -0.5, 0.09375, ((0, 16),), (0, 1, 16, 2.0))
    down_weight = noise(own_keys[4], (FF, D), FF ** -0.5, 0.046875, ((0, 16),))
    return dict(layer_input=layer_input, output_grad=output_grad, gate_weight=gate_weight, up_weight=up_weight, down_weight=down_weight)


def reference(layer_input, output_grad, gate_weight, up_weight, down_weight):
    gate_pre = jnp.dot(gate_weight, layer_input, preferred_element_type=jnp.float32)
    up_pre = jnp.dot(up_weight, layer_input, preferred_element_type=jnp.float32)
    sig = jax.nn.sigmoid(gate_pre)
    act = gate_pre * sig
    hidden_act = (act * up_pre).astype(jnp.bfloat16)
    hidden_grad = jnp.dot(down_weight, output_grad, preferred_element_type=jnp.float32)
    grad_gate_pre = (hidden_grad * up_pre * sig * (1.0 + gate_pre * (1.0 - sig))).astype(jnp.bfloat16)
    grad_up_pre = (hidden_grad * act).astype(jnp.bfloat16)
    down_grad = jnp.dot(hidden_act, output_grad.T, preferred_element_type=jnp.float32).astype(jnp.bfloat16)
    gate_grad = jnp.dot(grad_gate_pre, layer_input.T, preferred_element_type=jnp.float32).astype(jnp.bfloat16)
    up_grad = jnp.dot(grad_up_pre, layer_input.T, preferred_element_type=jnp.float32).astype(jnp.bfloat16)
    input_grad = jnp.dot(gate_weight.T, grad_gate_pre, preferred_element_type=jnp.float32)
    input_grad = input_grad + jnp.dot(up_weight.T, grad_up_pre, preferred_element_type=jnp.float32)
    return input_grad.astype(jnp.bfloat16), gate_grad, up_grad, down_grad
```

```python
import functools

import jax
import jax.numpy as jnp
from jax import lax
from jax.experimental import pallas as pl
from jax.experimental.pallas import tpu as pltpu
from jax.sharding import PartitionSpec as P

MESH = pl.DeviceIdType.MESH
VMEM_LIMIT = 64 * 1000 * 1000


def over_tokens(first_mat, second_mat):
    return lax.dot_general(
        first_mat, second_mat, (((1,), (1,)), ((), ())), preferred_element_type=jnp.float32
    )


def nearest(rank, here, extent):
    low = jnp.minimum(here, extent - 1 - here)
    half = (rank + 1) // 2
    both = jnp.where(rank % 2 == 1, here + half, here - half)
    one = jnp.where(here < extent - 1 - here, rank, extent - 1 - rank)
    return jnp.where(rank <= 2 * low, both, one)


def place(zs, xs):
    me = lax.axis_index("row")
    core = me % 2
    x = (me // 2) % xs
    z = me // (2 * xs)
    return z, x, core


def chip_at(step, z, x, zs, xs):
    cz = nearest(step // xs, z, zs)
    cx = nearest(step % xs, x, xs)
    return cz, cx, cz * xs + cx


def greet(z, x, core, zs, xs):
    barrier = pltpu.get_barrier_semaphore()

    def hail(cz, cx, cc):
        pl.semaphore_signal(
            barrier, inc=1, device_id={"row": (cz * xs + cx) * 2 + cc}, device_id_type=MESH
        )

    hail(z, x, 1 - core)
    pl.when(z > 0)(lambda: hail(z - 1, x, core))
    pl.when(z < zs - 1)(lambda: hail(z + 1, x, core))
    pl.when(x > 0)(lambda: hail(z, x - 1, core))
    pl.when(x < xs - 1)(lambda: hail(z, x + 1, core))
    count = 1 + jnp.minimum(z, 1) + jnp.minimum(zs - 1 - z, 1)
    count = count + jnp.minimum(x, 1) + jnp.minimum(xs - 1 - x, 1)
    pl.semaphore_wait(barrier, count)


def forward_kernel(
    zs, xs, x_ref, dy_ref, wg_ref, wu_ref, wd_ref,
    hact_ref, ggp_ref, gup_ref, xg_ref, dyg_ref,
    held, wbuf, acc, send_sem, recv_sem, wsem, own_sem, out_sem,
):
    z, x, core = place(zs, xs)
    mine = z * xs + x
    chips = zs * xs
    rows, hidden = held.shape[3], acc.shape[1]
    width = 2 * rows
    tokens = held.shape[4]

    def weights(step, fn):
        _, _, chip = chip_at(step, z, x, zs, xs)
        cols = pl.ds(pl.multiple_of(chip * width, 128), width)
        slot = step % 2
        for n, ref in enumerate((wg_ref, wu_ref, wd_ref)):
            fn(pltpu.make_async_copy(ref.at[:, cols], wbuf.at[slot, n], wsem.at[slot, n]))

    weights(0, lambda c: c.start())
    own = [
        pltpu.make_async_copy(ref, held.at[mine, n, core], own_sem.at[n])
        for n, ref in enumerate((x_ref, dy_ref))
    ]
    for c in own:
        c.start()
    greet(z, x, core, zs, xs)
    for c in own:
        c.wait()

    def passing(step, fn):
        cz, cx, chip = chip_at(step, z, x, zs, xs)
        block = held.at[chip, :, core]

        def copy(tz, tx, tc, n):
            return lambda: fn(
                pltpu.make_async_remote_copy(
                    src_ref=block,
                    dst_ref=block,
                    send_sem=send_sem.at[n, chip],
                    recv_sem=recv_sem.at[chip, core],
                    device_id={"row": (tz * xs + tx) * 2 + tc},
                    device_id_type=MESH,
                )
            )

        pl.when((cx == x) & (cz <= z) & (z < zs - 1))(copy(z + 1, x, core, 0))
        pl.when((cx == x) & (cz >= z) & (z > 0))(copy(z - 1, x, core, 1))
        pl.when((cx <= x) & (x < xs - 1))(copy(z, x + 1, core, 2))
        pl.when((cx >= x) & (x > 0))(copy(z, x - 1, core, 3))
        copy(z, x, 1 - core, 4)()

    def arrive(step, which):
        _, _, chip = chip_at(step, z, x, zs, xs)
        block = held.at[chip, :, which]
        pltpu.make_async_copy(block, block, recv_sem.at[chip, which]).wait()

    passing(0, lambda c: c.start())
    acc[...] = jnp.zeros_like(acc)

    def body(step, carry):
        @pl.when(step + 1 < chips)
        def _():
            weights(step + 1, lambda c: c.start())
            arrive(step + 1, core)
            passing(step + 1, lambda c: c.start())

        arrive(step, 1 - core)
        weights(step, lambda c: c.wait())
        _, _, chip = chip_at(step, z, x, zs, xs)
        for n, ref in enumerate((xg_ref, dyg_ref)):
            pltpu.make_async_copy(held.at[chip, n], ref.at[chip], out_sem.at[n, chip]).start()
        slot = step % 2
        x_block = held[chip, 0].reshape(width, tokens)
        acc[0] += jnp.dot(wbuf[slot, 0], x_block, preferred_element_type=jnp.float32)
        acc[1] += jnp.dot(wbuf[slot, 1], x_block, preferred_element_type=jnp.float32)
        dy_block = held[chip, 1].reshape(width, tokens)
        acc[2] += jnp.dot(wbuf[slot, 2], dy_block, preferred_element_type=jnp.float32)
        return carry

    lax.fori_loop(0, chips, body, 0)

    part = 112 if hidden % 112 == 0 else hidden

    def finish(n, carry):
        at = pl.ds(pl.multiple_of(n * part, 16), part)
        gate_pre, up_pre, hidden_grad = acc[0, at], acc[1, at], acc[2, at]
        sig = jax.nn.sigmoid(gate_pre)
        act = gate_pre * sig
        hact_ref[at] = (act * up_pre).astype(jnp.bfloat16)
        ggp_ref[at] = (
            hidden_grad * up_pre * sig * (1.0 + gate_pre * (1.0 - sig))
        ).astype(jnp.bfloat16)
        gup_ref[at] = (hidden_grad * act).astype(jnp.bfloat16)
        return carry

    lax.fori_loop(0, hidden // part, finish, 0)

    def drain(step, carry):
        _, _, chip = chip_at(step, z, x, zs, xs)
        passing(step, lambda c: c.wait_send())
        for n, ref in enumerate((xg_ref, dyg_ref)):
            pltpu.make_async_copy(held.at[chip, n], ref.at[chip], out_sem.at[n, chip]).wait()
        return carry

    lax.fori_loop(0, chips, drain, 0)


def scatter_kernel(
    zs, xs, ggp_ref, gup_ref, wg_ref, wu_ref, out_ref,
    wbuf, part, core_out, core_in, line_out, x_in, z_in,
    wsem, core_send, core_recv, line_send, x_recv, z_recv,
):
    z, x, core = place(zs, xs)
    chips = zs * xs
    rows, tokens = out_ref.shape
    width = 2 * rows

    def chip_of(step):
        return chip_at(chips - 1 - step, z, x, zs, xs)

    def weights(step, fn):
        _, _, chip = chip_of(step)
        cols = pl.ds(pl.multiple_of(chip * width, 128), width)
        slot = step % 2
        for n, ref in enumerate((wg_ref, wu_ref)):
            fn(pltpu.make_async_copy(ref.at[:, cols], wbuf.at[slot, n], wsem.at[slot, n]))

    def to_core(chip):
        return pltpu.make_async_remote_copy(
            src_ref=core_out.at[chip],
            dst_ref=core_in.at[chip],
            send_sem=core_send.at[chip],
            recv_sem=core_recv.at[chip],
            device_id={"row": (z * xs + x) * 2 + 1 - core},
            device_id_type=MESH,
        )

    def line(chip, tz, tx, buf, sems, side):
        return pltpu.make_async_remote_copy(
            src_ref=line_out.at[chip],
            dst_ref=buf.at[side, chip],
            send_sem=line_send.at[chip],
            recv_sem=sems.at[side, chip],
            device_id={"row": (tz * xs + tx) * 2 + core},
            device_id_type=MESH,
        )

    def onward(cz, cx, chip, fn):
        pl.when(cx > x)(lambda: fn(line(chip, z, x + 1, x_in, x_recv, 0)))
        pl.when(cx < x)(lambda: fn(line(chip, z, x - 1, x_in, x_recv, 1)))
        pl.when((cx == x) & (cz > z))(lambda: fn(line(chip, z + 1, x, z_in, z_recv, 0)))
        pl.when((cx == x) & (cz < z))(lambda: fn(line(chip, z - 1, x, z_in, z_recv, 1)))

    weights(0, lambda c: c.start())
    greet(z, x, core, zs, xs)

    def make(step):
        slot = step % 2
        _, _, chip = chip_of(step)

        @pl.when(step + 1 < chips)
        def _():
            weights(step + 1, lambda c: c.start())

        weights(step, lambda c: c.wait())
        total = jnp.dot(ggp_ref[...], wbuf[slot, 0], preferred_element_type=jnp.float32)
        total += jnp.dot(gup_ref[...], wbuf[slot, 1], preferred_element_type=jnp.float32)
        part[slot] = total.T.reshape(2, rows, tokens)
        core_out[chip] = part[slot, 1 - core].astype(jnp.bfloat16)
        to_core(chip).start()

    def add(step):
        slot = step % 2
        cz, cx, chip = chip_of(step)
        to_core(chip).wait_recv()
        part[slot, core] += core_in[chip].astype(jnp.float32)

        def take(buf, sems, side):
            def run():
                block = buf.at[side, chip]
                pltpu.make_async_copy(block, block, sems.at[side, chip]).wait()
                part[slot, core] += buf[side, chip].astype(jnp.float32)

            return run

        pl.when((cx >= x) & (x > 0))(take(x_in, x_recv, 0))
        pl.when((cx <= x) & (x < xs - 1))(take(x_in, x_recv, 1))
        pl.when((cx == x) & (cz >= z) & (z > 0))(take(z_in, z_recv, 0))
        pl.when((cx == x) & (cz <= z) & (z < zs - 1))(take(z_in, z_recv, 1))
        line_out[chip] = part[slot, core].astype(jnp.bfloat16)
        onward(cz, cx, chip, lambda c: c.start())

    make(0)

    def body(step, carry):
        make(step)
        add(step - 1)
        return carry

    lax.fori_loop(1, chips, body, 0)
    add(chips - 1)
    out_ref[...] = line_out[z * xs + x]

    def drain(step, carry):
        cz, cx, chip = chip_of(step)
        to_core(chip).wait_send()
        onward(cz, cx, chip, lambda c: c.wait_send())
        return carry

    lax.fori_loop(0, chips, drain, 0)


def on_device(zs, xs, layer_input, output_grad, gate_weight, up_weight, down_weight):
    chips = zs * xs
    rows, tokens = layer_input.shape
    hidden, features = gate_weight.shape
    width = 2 * rows
    bf16, f32 = jnp.bfloat16, jnp.float32
    anywhere = pl.BlockSpec(memory_space=pl.ANY)
    vmem = pl.BlockSpec(memory_space=pltpu.VMEM)
    DMA = pltpu.SemaphoreType.DMA
    small = jax.ShapeDtypeStruct((hidden, tokens), bf16)
    whole = jax.ShapeDtypeStruct((chips, 2, rows, tokens), bf16)
    hidden_act, ggp, gup, xg, dyg = pl.pallas_call(
        functools.partial(forward_kernel, zs, xs),
        out_shape=(small, small, small, whole, whole),
        in_specs=[anywhere] * 5,
        out_specs=(vmem, vmem, vmem, anywhere, anywhere),
        scratch_shapes=[
            pltpu.VMEM((chips, 2, 2, rows, tokens), bf16),
            pltpu.VMEM((2, 3, hidden, width), bf16),
            pltpu.VMEM((3, hidden, tokens), f32),
            DMA((5, chips)),
            DMA((chips, 2)),
            DMA((2, 3)),
            DMA((2,)),
            DMA((2, chips)),
        ],
        compiler_params=pltpu.CompilerParams(
            collective_id=0, has_side_effects=True, vmem_limit_bytes=VMEM_LIMIT
        ),
        name="gather_forward",
    )(layer_input, output_grad, gate_weight, up_weight, down_weight)
    input_grad = pl.pallas_call(
        functools.partial(scatter_kernel, zs, xs),
        out_shape=jax.ShapeDtypeStruct((rows, tokens), bf16),
        in_specs=[vmem, vmem, anywhere, anywhere],
        out_specs=vmem,
        scratch_shapes=[
            pltpu.VMEM((2, 2, hidden, width), bf16),
            pltpu.VMEM((2, 2, rows, tokens), f32),
            pltpu.VMEM((chips, rows, tokens), bf16),
            pltpu.VMEM((chips, rows, tokens), bf16),
            pltpu.VMEM((chips, rows, tokens), bf16),
            pltpu.VMEM((2, chips, rows, tokens), bf16),
            pltpu.VMEM((2, chips, rows, tokens), bf16),
            DMA((2, 2)),
            DMA((chips,)),
            DMA((chips,)),
            DMA((chips,)),
            DMA((2, chips)),
            DMA((2, chips)),
        ],
        compiler_params=pltpu.CompilerParams(
            collective_id=1, has_side_effects=True, vmem_limit_bytes=VMEM_LIMIT
        ),
        name="scatter_input_grad",
    )(ggp.T, gup.T, gate_weight, up_weight)
    block_in = xg.reshape(features, tokens)
    block_dy = dyg.reshape(features, tokens)
    down_grad = over_tokens(hidden_act, block_dy).astype(bf16)
    gate_grad = over_tokens(ggp, block_in).astype(bf16)
    up_grad = over_tokens(gup, block_in).astype(bf16)
    return (input_grad, gate_grad, up_grad, down_grad)


def solution(mesh):
    row = mesh.shape["row"]
    xs = 2 if row <= 16 else 4
    zs = row // (2 * xs)
    return jax.shard_map(
        functools.partial(on_device, zs, xs),
        mesh=mesh,
        in_specs=(
            P("row", "groups"),
            P("row", "groups"),
            P(("groups", "row"), None),
            P(("groups", "row"), None),
            P(("groups", "row"), None),
        ),
        out_specs=(
            P("row", "groups"),
            P(("groups", "row"), None),
            P(("groups", "row"), None),
            P(("groups", "row"), None),
        ),
        check_vma=False,
    )
```
